32 devices in a mesh: spec: 4 (over y, x), space: 8 (over z, core).
Axes of the slice: x: 2, y: 2, z: 4, core: 2. Of those that a mesh axis runs over, the one named last changes fastest.
Arguments:
- spectrum: float32 [1296, 32, 1024], P('spec', 'space'), may hold values from 0.05 to 2
- wind: float32 [2, 32, 1024], P(None, 'space'), may hold values from -5 to 5
- courant: float32 [2, 1296], P(None, 'spec'), may hold values from -0.5 to 0.5
- transfer: bfloat16 [1296, 1296], replicated
- sea_cells: int32 [8, 1920], P('space'), may hold values from 0 to 4095, as said below
Outputs:
- spectrum_out: float32 [1296, 32, 1024], P('spec', 'space')
The draws below stay inside these ranges and needn't reach their ends.
Inputs may be any that keep to these rules, and one draw needn't show every extreme that they name: `sea_cells`: each row lists the 1920 sea cells of one slab in ascending order, each once. Cut a slab's 4 * 1024 flattened cells into 4 aligned tiles of 1024 cells: a quarter of the tiles hold 1024 sea cells, a quarter 1024 // 2, a quarter 1024 // 4 and a quarter 1024 // 8, in an order drawn from the seed; the sea cells of a tile are its first ones.
All inputs are finite; a program needn't handle non-finite values.
Results may differ from the reference program's by a relative error of at most 0.0011.
Values sent between devices are 32-bit elements; how exact they have to be, the bound alone decides.
A program may use at most 128 MiB of HBM per device.

```python
import math
import jax
import jax.numpy as jnp
from jax import lax

NDIR = 36
NFREQ = 36
K = 1296
ROWS_DEV = 4
NY = 1024
SUB = 4
SRC_STEPS = 4
NX = 32
SLAB_SEA = 1920
N_SPEC = 4
N_SPACE = 8


def draw_transfer(key, part):
    first, second = jax.random.split(jax.random.fold_in(key, 5))
    off = jax.random.uniform(first, (K, K), jnp.float32, -0.0065, 0.0065)
    diag = jax.random.uniform(second, (K,), jnp.float32, -0.4, -0.2)
    rows = jnp.arange(K, dtype=jnp.int32)[:, None]
    cols = jnp.arange(K, dtype=jnp.int32)[None, :]
    eye = jnp.where(rows == cols, 1.0, 0.0).astype(jnp.float32)
    return (off * (1.0 - eye) + eye * diag[None, :]).astype(jnp.bfloat16)


def draw_courant(key, part):
    key_magnitude, key_sign, key_across = jax.random.split(jax.random.fold_in(key, 7), 3)
    magnitude = jax.random.uniform(key_magnitude, (K,), jnp.float32, 0.45, 0.5)
    direction_sign = (2 * jax.random.randint(key_sign, (K,), 0, 2) - 1).astype(jnp.float32)
    across = jax.random.uniform(key_across, (K,), jnp.float32, -0.45, 0.45)
    return jnp.stack([magnitude * direction_sign, across], axis=0)


def slab_list(key):
    tile = ROWS_DEV * NY // N_SPEC
    cells = ROWS_DEV * NY
    pattern = jnp.array([tile, tile // 2, tile // 4, tile // 8], jnp.int32)
    base = jnp.tile(pattern, N_SPEC // 4)
    counts = jax.random.permutation(key, base)
    ranks = jnp.arange(tile, dtype=jnp.int32)[None, :]
    sea = (ranks < counts[:, None]).reshape(cells)
    score = jnp.where(sea, 0, cells) + jnp.arange(cells, dtype=jnp.int32)
    return jnp.argsort(score)[:SLAB_SEA].astype(jnp.int32)


def draw_sea_cells(key, part):
    keys = jax.random.split(jax.random.fold_in(key, 11), N_SPACE)
    return jax.vmap(slab_list)(keys)


def steps_of(own_key, dims, shards, smallest, high):
    loudness, own = 1.0, jax.random.fold_in(own_key, 6)
    for dim, blocks in shards:
        draws = jnp.exp(jax.random.uniform(jax.random.fold_in(own, dim), (blocks,), jnp.float32, smallest / len(shards), high / len(shards)))
        loudness = loudness * jnp.repeat(draws, dims[dim] // blocks).reshape([-1 if axis == dim else 1 for axis in range(len(dims))])
    return loudness


def centred(key, shape, width, bound, cuts=(), held_as=jnp.bfloat16):
    level = steps_of(key, shape, cuts, -0.22, 0.18) if cuts else 1.0
    entries = jax.random.normal(key, shape, jnp.float32) * width * level
    return jnp.minimum(jnp.maximum(entries, -bound), bound).astype(held_as)


def setup_inputs(seed: int = 0) -> dict:
    key_of = jax.random.split(jax.random.key(seed), 6)
    spectrum = jnp.clip(jnp.exp(math.log(2.0) - 3.6888794 * jax.random.uniform(key_of[0], (K, NX, NY), jnp.float32) ** steps_of(key_of[0], (K, NX, NY), ((0, 4), (1, 8)), -0.2, 0.2)), 0.05, 2.0)
    wind = centred(key_of[1], (2, NX, NY), 1.0, 5.0, ((1, 8),), jnp.float32)
    courant = draw_courant(jax.random.fold_in(key_of[5], 71), 0)
    transfer = draw_transfer(jax.random.fold_in(key_of[5], 71), 0)
    sea_cells = draw_sea_cells(jax.random.fold_in(key_of[5], 71), 0)
    return {"spectrum": spectrum, "wind": wind, "courant": courant, "transfer": transfer, "sea_cells": sea_cells}


growth_rate = 0.05
whitecap = 0.1


def source_terms(points, wind_pts, transfer):
    angle = jnp.arange(NDIR, dtype=jnp.float32) * (2.0 * math.pi / NDIR)
    cos_comp = jnp.repeat(jnp.cos(angle), NFREQ)
    sin_comp = jnp.repeat(jnp.sin(angle), NFREQ)
    growth = jnp.tile(growth_rate * (jnp.arange(NFREQ, dtype=jnp.float32) + 1.0) / NFREQ, NDIR)
    drive = jnp.maximum(cos_comp[:, None] * wind_pts[0][None, :] + sin_comp[:, None] * wind_pts[1][None, :], 0.0)
    gamma = growth[:, None] * drive
    for step in range(SRC_STEPS):
        low = points.astype(jnp.bfloat16)
        moved = jnp.dot(transfer, low, preferred_element_type=jnp.float32)
        mean = jnp.mean(points, axis=0, keepdims=True)
        points = points + (gamma - whitecap * mean) * points + moved
    return points


def advance(padded, cx, cy):
    centre = padded[:, 1:-1]
    upper = padded[:, :-2]
    lower = padded[:, 2:]
    left = jnp.roll(centre, 1, axis=2)
    right = jnp.roll(centre, -1, axis=2)
    return (centre - jnp.maximum(cx, 0.0) * (centre - upper) - jnp.minimum(cx, 0.0) * (lower - centre)
            - jnp.maximum(cy, 0.0) * (centre - left) - jnp.minimum(cy, 0.0) * (right - centre))


def reference(spectrum, wind, courant, transfer, sea_cells):
    cells = ROWS_DEV * NY
    flat = spectrum.reshape(K, N_SPACE, cells)
    wind_flat = wind.reshape(2, N_SPACE, cells)

    def one_slab(slab):
        index_list = sea_cells[slab]
        block = lax.dynamic_index_in_dim(flat, slab, 1, keepdims=False)
        wind_block = lax.dynamic_index_in_dim(wind_flat, slab, 1, keepdims=False)
        points = jnp.take(block, index_list, axis=1)
        wind_pts = jnp.take(wind_block, index_list, axis=1)
        points = source_terms(points, wind_pts, transfer)
        return jnp.zeros((K, cells), jnp.float32).at[:, index_list].set(points)

    slabs = lax.map(one_slab, jnp.arange(N_SPACE, dtype=jnp.int32))
    energy = slabs.transpose(1, 0, 2).reshape(K, NX, NY)
    offsets = (jnp.arange(N_SPACE, dtype=jnp.int32) * cells)[:, None]
    positions = (sea_cells + offsets).reshape(-1)
    mask = jnp.zeros((N_SPACE * cells,), jnp.float32).at[positions].set(1.0).reshape(1, NX, NY)
    cx = courant[0][:, None, None]
    cy = courant[1][:, None, None]
    for step in range(SUB):
        padded = jnp.pad(energy, ((0, 0), (1, 1), (0, 0)))
        energy = advance(padded, cx, cy) * mask
    return energy
```

```python
import math

import jax
import jax.numpy as jnp
import numpy as np
from jax import lax
from jax.experimental import pallas as pl
from jax.experimental.pallas import tpu as pltpu
from jax.sharding import PartitionSpec as P

NDIR = 36
NFREQ = 36
SUB = 4
SRC_STEPS = 4


growth_rate = 0.05
whitecap = 0.1


def padded_2(cells, sides, width):
    for axis, dim in sides:
        count = lax.axis_size(axis)
        ends = count - 1
        head = lax.slice_in_dim(cells, 0, width, axis=dim)
        tail = lax.slice_in_dim(cells, cells.shape[dim] - width, cells.shape[dim], axis=dim)
        cells = jnp.concatenate(
            [
                lax.ppermute(tail, axis, [(i, (i + 1) % count) for i in range(ends)]),
                cells,
                lax.ppermute(head, axis, [((i + 1) % count, i) for i in range(ends)]),
            ],
            axis=dim,
        )
    return cells


def source_terms(points, wind_pts, transfer):
    angle = jnp.arange(NDIR, dtype=jnp.float32) * (2.0 * math.pi / NDIR)
    cos_comp = jnp.repeat(jnp.cos(angle), NFREQ)
    sin_comp = jnp.repeat(jnp.sin(angle), NFREQ)
    growth = jnp.tile(growth_rate * (jnp.arange(NFREQ, dtype=jnp.float32) + 1.0) / NFREQ, NDIR)
    drive = jnp.maximum(
        cos_comp[:, None] * wind_pts[0][None, :] + sin_comp[:, None] * wind_pts[1][None, :], 0.0
    )
    gamma = growth[:, None] * drive
    for step in range(SRC_STEPS):
        low = points.astype(jnp.bfloat16)
        moved = jnp.dot(transfer, low, preferred_element_type=jnp.float32)
        mean = jnp.mean(points, axis=0, keepdims=True)
        points = points + (gamma - whitecap * mean) * points + moved
    return points


def advance(padded, cx, cy):
    centre = padded[:, 1:-1]
    upper = padded[:, :-2]
    lower = padded[:, 2:]
    left = jnp.roll(centre, 1, axis=2)
    right = jnp.roll(centre, -1, axis=2)
    return (
        centre
        - jnp.maximum(cx, 0.0) * (centre - upper)
        - jnp.minimum(cx, 0.0) * (lower - centre)
        - jnp.maximum(cy, 0.0) * (centre - left)
        - jnp.minimum(cy, 0.0) * (right - centre)
    )


def body(spectrum, wind, courant, transfer, sea_cells):
    comps, rows, cols = spectrum.shape
    cells = rows * cols
    groups = lax.axis_size("spec")
    member = lax.axis_index("spec")
    sea_list = sea_cells[0]
    flat = spectrum.reshape(comps, cells)
    wind_flat = wind.reshape(2, cells)
    mask = jnp.zeros((cells,), jnp.float32).at[sea_list].set(1.0)
    tile = cells // groups
    masked = flat * mask[None, :]
    points = lax.all_to_all(masked, "spec", split_axis=1, concat_axis=0, tiled=True)
    wind_tile = lax.dynamic_slice_in_dim(wind_flat, member * tile, tile, 1)
    updated = source_terms(points, wind_tile, transfer)
    energy = lax.all_to_all(updated, "spec", split_axis=0, concat_axis=1, tiled=True)
    field = energy.reshape(comps, rows, cols)
    cx = courant[0][:, None, None]
    cy = courant[1][:, None, None]
    mask_rows = mask.reshape(1, rows, cols)
    for step in range(SUB):
        padded = padded_2(field, (("space", 1),), 1)
        field = advance(padded, cx, cy) * mask_rows
    return field


LANES = 128
MESH = pl.DeviceIdType.MESH


def fits(mesh, spectrum, wind, courant, transfer, sea_cells):
    groups = mesh.shape["spec"]
    cells = spectrum.shape[1] * spectrum.shape[2]
    tile = cells // groups
    return (
        groups == 4
        and tile % (8 * LANES) == 0
        and spectrum.shape[2] % LANES == 0
        and sea_cells.shape[1] == 15 * LANES
        and spectrum.shape[1] == SUB
    )


def compact_kernel(sea, spectrum, wind, blocks, winds, sem, wind_sem):
    per_row = spectrum.shape[2] // LANES
    count = blocks.shape[0]
    copies = []
    for q in range(count - 1):
        place = lax.div(sea[0, q * LANES], LANES)
        row = lax.div(place, per_row)
        col = pl.multiple_of(lax.rem(place, per_row) * LANES, LANES)
        copies.append(pltpu.make_async_copy(spectrum.at[:, row, pl.ds(col, LANES)], blocks.at[q], sem.at[q]))
        copies.append(pltpu.make_async_copy(wind.at[:, row, pl.ds(col, LANES)], winds.at[q], wind_sem.at[q]))
    for copy in copies:
        copy.start()
    blocks[count - 1] = jnp.zeros(blocks.shape[1:], blocks.dtype)
    winds[count - 1] = jnp.zeros(winds.shape[1:], winds.dtype)
    for copy in copies:
        copy.wait()


def relatives(s):
    return (s + 1 - 2 * lax.rem(s, 2), lax.rem(s + 2, 4), 3 - s)


def exchange_kernel(ends, blocks, winds, trig, transfer, out, came, points, low, gamma, made,
                    in_send, in_recv, out_send, out_recv, halo_send, halo_recv, own_sem, kept_sem):
    s = lax.axis_index("spec")
    z = lax.axis_index("space")
    peers = relatives(s)
    comps = blocks.shape[1]
    count = blocks.shape[0]
    chunks = count // 4
    total = points.shape[0]

    barrier = pltpu.get_barrier_semaphore()
    for peer in peers:
        pl.semaphore_signal(barrier, inc=1, device_id={"spec": peer}, device_id_type=MESH)

    @pl.when(z > 0)
    def _():
        pl.semaphore_signal(barrier, inc=1, device_id={"space": z - 1}, device_id_type=MESH)

    @pl.when(z < ends)
    def _():
        pl.semaphore_signal(barrier, inc=1, device_id={"space": z + 1}, device_id_type=MESH)

    pl.semaphore_wait(barrier, 3 + jnp.minimum(z, 1) + jnp.minimum(ends - z, 1))

    def inward(c, j, sending):
        source = blocks.at[chunks * peers[j] + c]
        target = came.at[c, s if sending else peers[j]]
        return pltpu.make_async_remote_copy(
            src_ref=source, dst_ref=target, send_sem=in_send.at[c, j], recv_sem=in_recv.at[c, j],
            device_id={"spec": peers[j]}, device_id_type=MESH)

    def outward(c, j, sending):
        source = made.at[c, peers[j]]
        target = out.at[count + chunks * (s if sending else peers[j]) + c]
        return pltpu.make_async_remote_copy(
            src_ref=source, dst_ref=target, send_sem=out_send.at[c, j], recv_sem=out_recv.at[c, j],
            device_id={"spec": peers[j]}, device_id_type=MESH)

    def own(c):
        return pltpu.make_async_copy(blocks.at[chunks * s + c], came.at[c, s], own_sem.at[c])

    def kept(c):
        return pltpu.make_async_copy(made.at[c, s], out.at[count + chunks * s + c], kept_sem.at[c])

    def halo(q, way):
        return pltpu.make_async_remote_copy(
            src_ref=out.at[count + q], dst_ref=out.at[q + 2 * way * count],
            send_sem=halo_send.at[way, q], recv_sem=halo_recv.at[way, q],
            device_id={"space": z + 1 - 2 * way}, device_id_type=MESH)

    for c in range(chunks):
        own(c).start()
        for j in (2, 0, 1):
            inward(c, j, True).start()

    def chunk(c, carry):
        own(c).wait()
        for j in range(3):
            inward(c, j, False).wait_recv()
        for p in range(4):
            points[p * comps:(p + 1) * comps, :] = came[c, p]
        pair = winds[chunks * s + c]
        drive = jnp.maximum(trig[:, 0:1] * pair[0:1, :] + trig[:, 1:2] * pair[1:2, :], 0.0)
        gamma[...] = trig[:, 2:3] * drive

        def source(step, carry):
            e = points[...]
            low[...] = e.astype(jnp.bfloat16)
            mean = jnp.sum(e, axis=0, keepdims=True) * (1.0 / total)
            moved = jnp.dot(transfer[...], low[...], preferred_element_type=jnp.float32)
            points[...] = e + (gamma[...] - whitecap * mean) * e + moved
            return carry

        lax.fori_loop(0, SRC_STEPS, source, 0)
        for p in range(4):
            made[c, p] = points[p * comps:(p + 1) * comps, :]
        for j in (2, 0, 1):
            outward(c, j, True).start()
        kept(c).start()
        return carry

    lax.fori_loop(0, chunks, chunk, 0)

    def send_halo(q):
        @pl.when(z < ends)
        def _():
            halo(q, 0).start()

        @pl.when(z > 0)
        def _():
            halo(q, 1).start()

    def spread(c, carry):
        kept(c).wait()
        send_halo(chunks * s + c)
        for j in range(3):
            outward(c, j, False).wait_recv()
            send_halo(chunks * peers[j] + c)
        return carry

    lax.fori_loop(0, chunks, spread, 0)

    def finish(c, carry):
        for j in range(3):
            inward(c, j, True).wait_send()
            outward(c, j, True).wait_send()
        return carry

    lax.fori_loop(0, chunks, finish, 0)

    def finish_halo(q, carry):
        @pl.when(z < ends)
        def _():
            halo(q, 0).wait_send()
            halo(q, 1).wait_recv()

        @pl.when(z > 0)
        def _():
            halo(q, 1).wait_send()
            halo(q, 0).wait_recv()

        return carry

    lax.fori_loop(0, count, finish_halo, 0)


def advance_kernel(ends, sea, blocks, coef, out, first, second, bank, table, places, sems, zero_sem):
    z = lax.axis_index("space")
    comps = coef.shape[0]
    count = blocks.shape[0] // 3
    rows, per_row = out.shape[1], out.shape[2] // LANES
    span = rows * per_row
    empty = 2 * count - 1
    live = count - 1

    def clear(i, carry):
        table[i] = empty
        return carry

    lax.fori_loop(0, (3 * rows + 2) * per_row, clear, 0)
    for slab in range(3):
        present = jnp.logical_and(z + slab - 1 >= 0, z + slab - 1 <= ends)

        def note(q, carry):
            place = lax.div(sea[slab, q * LANES], LANES) + slab * span
            places[slab * live + q] = place

            @pl.when(present)
            def _():
                table[per_row + place] = slab * count + q

            return carry

        lax.fori_loop(0, live, note, 0)

    cx = coef[:, 0:1]
    cy = coef[:, 1:2]
    wide = (comps, LANES)
    bank[0] = jnp.broadcast_to(1.0 - jnp.abs(cx) - jnp.abs(cy), wide)
    bank[1] = jnp.broadcast_to(jnp.maximum(cx, 0.0), wide)
    bank[2] = jnp.broadcast_to(-jnp.minimum(cx, 0.0), wide)
    bank[3] = jnp.broadcast_to(cy, wide)
    first[empty] = jnp.zeros(wide, jnp.float32)
    second[empty] = jnp.zeros(wide, jnp.float32)
    lane = lax.broadcasted_iota(jnp.int32, wide, 1)

    def write(i):
        row = lax.div(i, per_row)
        col = pl.multiple_of(lax.rem(i, per_row) * LANES, LANES)
        return row, col

    for step in range(SUB):
        old = blocks if step == 0 else (first, second)[(step + 1) % 2]
        new = (first, second)[step % 2]

        def one(n, carry):
            place = places[n]
            row = lax.div(place, per_row)
            col = lax.rem(place, per_row)
            mine = table[per_row + place]
            due = jnp.logical_and(jnp.logical_and(row >= 1 + step, row <= 3 * rows - 2 - step), mine != empty)

            @pl.when(due)
            def _():
                start = per_row + row * per_row
                left = table[start + lax.rem(col + per_row - 1, per_row)]
                right = table[start + lax.rem(col + 1, per_row)]
                e = old[mine]
                to_right = pltpu.roll(jnp.where(lane == LANES - 1, old[left], e), 1, 1)
                to_left = pltpu.roll(jnp.where(lane == 0, old[right], e), LANES - 1, 1)
                across = bank[3]
                side = jnp.where(across > 0.0, to_right, to_left)
                new[mine] = (bank[0] * e + bank[1] * old[table[place]] + bank[2] * old[table[place + 2 * per_row]]
                             + jnp.abs(across) * side)

            return carry

        lax.fori_loop(0, 3 * live, one, 0)

    final = (first, second)[(SUB - 1) % 2]

    def put(i):
        row, col = write(i)
        return pltpu.make_async_copy(
            final.at[table[per_row + span + i]], out.at[:, row, pl.ds(col, LANES)], sems.at[i])

    lax.fori_loop(0, span, lambda i, c: (put(i).start(), c)[1], 0)
    lax.fori_loop(0, span, lambda i, c: (put(i).wait(), c)[1], 0)


def fast_body(spectrum, wind, courant, transfer, sea_cells):
    comps, rows, cols = spectrum.shape
    total = transfer.shape[0]
    count = sea_cells.shape[1] // LANES + 1
    chunks = count // 4
    ends = lax.axis_size("space") - 1
    dma = pltpu.SemaphoreType.DMA
    vmem = pl.BlockSpec(memory_space=pltpu.VMEM)
    smem = pl.BlockSpec(memory_space=pltpu.SMEM)
    hbm = pl.BlockSpec(memory_space=pl.ANY)
    f32 = jnp.float32

    above = lax.ppermute(sea_cells, "space", [(i, i + 1) for i in range(ends)])
    below = lax.ppermute(sea_cells, "space", [(i + 1, i) for i in range(ends)])
    seas = jnp.concatenate([above, sea_cells, below], axis=0)

    blocks, winds = pl.pallas_call(
        compact_kernel,
        out_shape=(jax.ShapeDtypeStruct((count, comps, LANES), f32), jax.ShapeDtypeStruct((count, 2, LANES), f32)),
        in_specs=[smem, hbm, hbm],
        out_specs=(vmem, vmem),
        scratch_shapes=[dma((count,)), dma((count,))],
        name="compact",
    )(sea_cells, spectrum, wind)

    angle = np.arange(NDIR, dtype=np.float32) * np.float32(2.0 * math.pi / NDIR)
    growth = np.float32(growth_rate) * (np.arange(NFREQ, dtype=np.float32) + 1.0) / NFREQ
    trig = jnp.asarray(np.stack([
        np.repeat(np.cos(angle), NFREQ), np.repeat(np.sin(angle), NFREQ), np.tile(growth, NDIR)], axis=1), f32)

    slabs = pl.pallas_call(
        lambda *refs: exchange_kernel(ends, *refs),
        out_shape=jax.ShapeDtypeStruct((3 * count, comps, LANES), f32),
        in_specs=[vmem, vmem, vmem, vmem],
        out_specs=hbm,
        scratch_shapes=[
            pltpu.VMEM((chunks, 4, comps, LANES), f32),
            pltpu.VMEM((total, LANES), f32),
            pltpu.VMEM((total, LANES), jnp.bfloat16),
            pltpu.VMEM((total, LANES), f32),
            pltpu.VMEM((chunks, 4, comps, LANES), f32),
            dma((chunks, 3)), dma((chunks, 3)), dma((chunks, 3)), dma((chunks, 3)),
            dma((2, count)), dma((2, count)), dma((chunks,)), dma((chunks,)),
        ],
        compiler_params=pltpu.CompilerParams(collective_id=0, has_side_effects=True, vmem_limit_bytes=48 << 20),
        name="exchange",
    )(blocks, winds, trig, transfer)

    return pl.pallas_call(
        lambda *refs: advance_kernel(ends, *refs),
        out_shape=jax.ShapeDtypeStruct(spectrum.shape, f32),
        in_specs=[smem, vmem, vmem],
        out_specs=hbm,
        scratch_shapes=[
            pltpu.VMEM((3 * count, comps, LANES), f32),
            pltpu.VMEM((3 * count, comps, LANES), f32),
            pltpu.VMEM((4, comps, LANES), f32),
            pltpu.SMEM(((3 * rows + 2) * (cols // LANES),), jnp.int32),
            pltpu.SMEM((3 * count,), jnp.int32),
            dma((rows * (cols // LANES),)), dma,
        ],
        compiler_params=pltpu.CompilerParams(vmem_limit_bytes=48 << 20),
        name="advance",
    )(seas, slabs, courant.T)


def solution(mesh):
    def step(*args):
        if fits(mesh, *args):
            return fast_body(*args)
        return body(*args)

    in_specs = (
        P("spec", "space", None),
        P(None, "space", None),
        P(None, "spec"),
        P(),
        P("space", None),
    )
    out_specs = P("spec", "space", None)
    return jax.shard_map(step, mesh=mesh, in_specs=in_specs, out_specs=out_specs, check_vma=False)
```

```python
import math

import jax
import jax.numpy as jnp
import numpy as np
from jax import lax
from jax.experimental import pallas as pl
from jax.experimental.pallas import tpu as pltpu
from jax.sharding import PartitionSpec as P

NDIR = 36
NFREQ = 36
SUB = 4
SRC_STEPS = 4


growth_rate = 0.05
whitecap = 0.1


def padded_2(cells, sides, width):
    for axis, dim in sides:
        count = lax.axis_size(axis)
        ends = count - 1
        head = lax.slice_in_dim(cells, 0, width, axis=dim)
        tail = lax.slice_in_dim(cells, cells.shape[dim] - width, cells.shape[dim], axis=dim)
        cells = jnp.concatenate(
            [
                lax.ppermute(tail, axis, [(i, (i + 1) % count) for i in range(ends)]),
                cells,
                lax.ppermute(head, axis, [((i + 1) % count, i) for i in range(ends)]),
            ],
            axis=dim,
        )
    return cells


def source_terms(points, wind_pts, transfer):
    angle = jnp.arange(NDIR, dtype=jnp.float32) * (2.0 * math.pi / NDIR)
    cos_comp = jnp.repeat(jnp.cos(angle), NFREQ)
    sin_comp = jnp.repeat(jnp.sin(angle), NFREQ)
    growth = jnp.tile(growth_rate * (jnp.arange(NFREQ, dtype=jnp.float32) + 1.0) / NFREQ, NDIR)
    drive = jnp.maximum(
        cos_comp[:, None] * wind_pts[0][None, :] + sin_comp[:, None] * wind_pts[1][None, :], 0.0
    )
    gamma = growth[:, None] * drive
    for step in range(SRC_STEPS):
        low = points.astype(jnp.bfloat16)
        moved = jnp.dot(transfer, low, preferred_element_type=jnp.float32)
        mean = jnp.mean(points, axis=0, keepdims=True)
        points = points + (gamma - whitecap * mean) * points + moved
    return points


def advance(padded, cx, cy):
    centre = padded[:, 1:-1]
    upper = padded[:, :-2]
    lower = padded[:, 2:]
    left = jnp.roll(centre, 1, axis=2)
    right = jnp.roll(centre, -1, axis=2)
    return (
        centre
        - jnp.maximum(cx, 0.0) * (centre - upper)
        - jnp.minimum(cx, 0.0) * (lower - centre)
        - jnp.maximum(cy, 0.0) * (centre - left)
        - jnp.minimum(cy, 0.0) * (right - centre)
    )


def body(spectrum, wind, courant, transfer, sea_cells):
    comps, rows, cols = spectrum.shape
    cells = rows * cols
    groups = lax.axis_size("spec")
    member = lax.axis_index("spec")
    sea_list = sea_cells[0]
    flat = spectrum.reshape(comps, cells)
    wind_flat = wind.reshape(2, cells)
    mask = jnp.zeros((cells,), jnp.float32).at[sea_list].set(1.0)
    tile = cells // groups
    masked = flat * mask[None, :]
    points = lax.all_to_all(masked, "spec", split_axis=1, concat_axis=0, tiled=True)
    wind_tile = lax.dynamic_slice_in_dim(wind_flat, member * tile, tile, 1)
    updated = source_terms(points, wind_tile, transfer)
    energy = lax.all_to_all(updated, "spec", split_axis=0, concat_axis=1, tiled=True)
    field = energy.reshape(comps, rows, cols)
    cx = courant[0][:, None, None]
    cy = courant[1][:, None, None]
    mask_rows = mask.reshape(1, rows, cols)
    for step in range(SUB):
        padded = padded_2(field, (("space", 1),), 1)
        field = advance(padded, cx, cy) * mask_rows
    return field


LANES = 128
NO_ROW = -5000
NO_COLUMN = -1000
GROUP = 56
MESH = pl.DeviceIdType.MESH


def fits(mesh, spectrum, wind, courant, transfer, sea_cells):
    groups = mesh.shape["spec"]
    cells = spectrum.shape[1] * spectrum.shape[2]
    tile = cells // groups
    return (
        groups == 4
        and tile % (8 * LANES) == 0
        and spectrum.shape[2] % LANES == 0
        and sea_cells.shape[1] == 15 * LANES
        and spectrum.shape[1] == SUB
    )


def compact_kernel(sea, spectrum, wind, blocks, winds, places, sem, wind_sem):
    per_row = spectrum.shape[2] // LANES
    count = blocks.shape[0]
    lane = lax.broadcasted_iota(jnp.int32, (8, LANES), 1)
    across = jnp.full((8, LANES), NO_ROW, jnp.int32)
    down = []
    copies = []
    for q in range(count - 1):
        place = lax.div(sea[0, q * LANES], LANES)
        row = lax.div(place, per_row)
        col = pl.multiple_of(lax.rem(place, per_row) * LANES, LANES)
        copies.append(pltpu.make_async_copy(spectrum.at[:, row, pl.ds(col, LANES)], blocks.at[q], sem.at[q]))
        copies.append(pltpu.make_async_copy(wind.at[:, row, pl.ds(col, LANES)], winds.at[q], wind_sem.at[q]))
        copies[-2].start()
        copies[-1].start()
        across = jnp.where(lane == q, place, across)
        places[8 + q:9 + q, :] = jnp.full((1, LANES), place, jnp.int32)
    places[0:8, :] = across
    places[7 + count:8 + count, :] = jnp.full((1, LANES), NO_COLUMN, jnp.int32)
    blocks[count - 1] = jnp.zeros(blocks.shape[1:], blocks.dtype)
    winds[count - 1] = jnp.zeros(winds.shape[1:], winds.dtype)
    for copy in copies:
        copy.wait()


def relatives(s):
    return (s + 1 - 2 * lax.rem(s, 2), lax.rem(s + 2, 4), 3 - s)


def cuts(comps):
    starts = list(range(0, comps - GROUP // 2, GROUP))
    return list(zip(starts, starts[1:] + [comps]))


def exchange_kernel(ends, per_row, span, blocks, winds, places, coef, trig_hbm, transfer_hbm, out, *scratch):
    groups = cuts(blocks.shape[1])
    fields = scratch[:len(groups)]
    results = scratch[len(groups):2 * len(groups)]
    (came, points, low, gamma, made, trig, transfer, bank, first, second, lists, found, table,
     in_send, in_recv, out_send, out_recv, halo_send, halo_recv, own_sem, kept_sem,
     list_send, list_recv, load_sem, result_sem) = scratch[2 * len(groups):]
    s = lax.axis_index("spec")
    z = lax.axis_index("space")
    peers = relatives(s)
    comps = blocks.shape[1]
    count = blocks.shape[0]
    chunks = count // 4
    total = points.shape[0]

    barrier = pltpu.get_barrier_semaphore()
    for peer in peers:
        pl.semaphore_signal(barrier, inc=1, device_id={"spec": peer}, device_id_type=MESH)

    @pl.when(z > 0)
    def _():
        pl.semaphore_signal(barrier, inc=1, device_id={"space": z - 1}, device_id_type=MESH)

    @pl.when(z < ends)
    def _():
        pl.semaphore_signal(barrier, inc=1, device_id={"space": z + 1}, device_id_type=MESH)

    pl.semaphore_wait(barrier, 3 + jnp.minimum(z, 1) + jnp.minimum(ends - z, 1))

    def inward(c, j, sending):
        source = blocks.at[chunks * peers[j] + c]
        target = came.at[c, s if sending else peers[j]]
        return pltpu.make_async_remote_copy(
            src_ref=source, dst_ref=target, send_sem=in_send.at[c, j], recv_sem=in_recv.at[c, j],
            device_id={"spec": peers[j]}, device_id_type=MESH)

    def outward(g, c, j, sending):
        source = made.at[c, peers[j], pl.ds(groups[g][0], groups[g][1] - groups[g][0])]
        target = fields[g].at[count + chunks * (s if sending else peers[j]) + c]
        return pltpu.make_async_remote_copy(
            src_ref=source, dst_ref=target, send_sem=out_send.at[g, c, j], recv_sem=out_recv.at[g, c, j],
            device_id={"spec": peers[j]}, device_id_type=MESH)

    def own(c):
        return pltpu.make_async_copy(blocks.at[chunks * s + c], came.at[c, s], own_sem.at[c])

    def kept(g, c):
        source = made.at[c, s, pl.ds(groups[g][0], groups[g][1] - groups[g][0])]
        return pltpu.make_async_copy(source, fields[g].at[count + chunks * s + c], kept_sem.at[g, c])

    def halo(g, part, d, way):
        return pltpu.make_async_remote_copy(
            src_ref=fields[g].at[pl.ds(count + chunks * d, chunks)],
            dst_ref=fields[g].at[pl.ds(2 * way * count + chunks * d, chunks)],
            send_sem=halo_send.at[g, way, part], recv_sem=halo_recv.at[g, way, part],
            device_id={"space": z + 1 - 2 * way}, device_id_type=MESH)

    def listed(way):
        return pltpu.make_async_remote_copy(
            src_ref=places, dst_ref=lists.at[way], send_sem=list_send.at[way], recv_sem=list_recv.at[way],
            device_id={"space": z + 1 - 2 * way}, device_id_type=MESH)

    def result(g):
        lo, hi = groups[g]
        return pltpu.make_async_copy(results[g], out.at[:, pl.ds(lo, hi - lo)], result_sem.at[g])

    loads = (pltpu.make_async_copy(trig_hbm, trig, load_sem.at[0]),
             pltpu.make_async_copy(transfer_hbm, transfer, load_sem.at[1]))

    for c in range(chunks):
        own(c).start()
        for j in (2, 0, 1):
            inward(c, j, True).start()

    for load in loads:
        load.start()

    @pl.when(z < ends)
    def _():
        listed(0).start()

    @pl.when(z > 0)
    def _():
        listed(1).start()

    @pl.when(z == 0)
    def _():
        for field in fields:
            field[0:count] = jnp.zeros((count,) + field.shape[1:], field.dtype)

    @pl.when(z == ends)
    def _():
        for field in fields:
            field[2 * count:3 * count] = jnp.zeros((count,) + field.shape[1:], field.dtype)

    wide = (comps, LANES)
    cx = coef[:, 0:1]
    cy = coef[:, 1:2]
    bank[0] = jnp.broadcast_to(1.0 - jnp.abs(cx) - jnp.abs(cy), wide)
    bank[1] = jnp.broadcast_to(jnp.maximum(cx, 0.0), wide)
    bank[2] = jnp.broadcast_to(-jnp.minimum(cx, 0.0), wide)
    bank[3] = jnp.broadcast_to(cy, wide)

    @pl.when(z < ends)
    def _():
        listed(1).wait_recv()

    @pl.when(z > 0)
    def _():
        listed(0).wait_recv()

    slabs = []
    for slab in range(3):
        if slab == 1:
            across, down = places[0:8, :], places[8:8 + count, :]
        else:
            there = z > 0 if slab == 0 else z < ends
            side = lists[slab // 2]
            across = jnp.where(there, side[0:8, :], NO_ROW)
            down = jnp.where(there, side[8:8 + count, :], NO_COLUMN)
        slabs.append((across, down + slab * span))
    empty = 2 * count - 1
    sub = lax.broadcasted_iota(jnp.int32, (count, LANES), 0)
    for slab, (across, _) in enumerate(slabs):
        place = across[0:1, :]
        col = lax.rem(place, per_row)
        base = place - col + slab * span
        goals = (base + lax.rem(col + per_row - 1, per_row), base + lax.rem(col + 1, per_row),
                 base + col - per_row, base + col + per_row)
        for k, goal in enumerate(goals):
            index = jnp.full((1, LANES), empty, jnp.int32)
            for other, (_, down) in enumerate(slabs):
                hit = jnp.where(down == goal, sub + (other * count - empty), 0)
                index = index + jnp.sum(hit, axis=0, keepdims=True)
            found[4 * slab + k:4 * slab + k + 1, :] = index
    found[12:16, :] = jnp.full((4, LANES), empty, jnp.int32)
    to_table = pltpu.make_async_copy(found, table, load_sem.at[2])
    to_table.start()
    to_table.wait()
    for load in loads:
        load.wait()

    def chunk(c, carry):
        own(c).wait()
        for j in range(3):
            inward(c, j, False).wait_recv()
        for p in range(4):
            points[p * comps:(p + 1) * comps, :] = came[c, p]
        pair = winds[chunks * s + c]
        drive = jnp.maximum(trig[:, 0:1] * pair[0:1, :] + trig[:, 1:2] * pair[1:2, :], 0.0)
        gamma[...] = trig[:, 2:3] * drive

        def source(step, carry):
            e = points[...]
            low[...] = e.astype(jnp.bfloat16)
            mean = jnp.sum(e, axis=0, keepdims=True) * (1.0 / total)
            moved = jnp.dot(transfer[...], low[...], preferred_element_type=jnp.float32)
            points[...] = e + (gamma[...] - whitecap * mean) * e + moved
            return carry

        lax.fori_loop(0, SRC_STEPS, source, 0)
        for p in range(4):
            made[c, p] = points[p * comps:(p + 1) * comps, :]
        for j in (2, 0, 1):
            outward(0, c, j, True).start()
        kept(0, c).start()
        return carry

    lax.fori_loop(0, chunks, chunk, 0)

    for g in range(1, len(groups)):
        def send(c, carry, g=g):
            for j in (2, 0, 1):
                outward(g, c, j, True).start()
            kept(g, c).start()
            return carry

        lax.fori_loop(0, chunks, send, 0)

    def send_halo(g):
        def send(part, d):
            @pl.when(z < ends)
            def _():
                halo(g, part, d, 0).start()

            @pl.when(z > 0)
            def _():
                halo(g, part, d, 1).start()

        for c in range(chunks):
            kept(g, c).wait()
        send(3, s)
        for j in range(3):
            for c in range(chunks):
                outward(g, c, j, False).wait_recv()
            send(j, peers[j])

    def take_halo(g):
        for part, d in enumerate(peers + (s,)):
            @pl.when(z < ends)
            def _():
                halo(g, part, d, 1).wait_recv()

            @pl.when(z > 0)
            def _():
                halo(g, part, d, 0).wait_recv()

    def advance_group(g):
        lo, hi = groups[g]
        size = hi - lo
        lane = lax.broadcasted_iota(jnp.int32, (size, LANES), 1)
        for step, lead in enumerate((1, 3, 7, count)):
            old = (fields[g], first, second, first)[step]
            new = (first, second, first, results[g])[step]
            last = 3 * count - 1 - lead if step < 3 else 2 * count - 1
            shift = count if step == 3 else 0

            def one(n, carry):
                slab = lax.div(n, count)
                q = lax.rem(n, count)
                left = table[4 * slab, q]
                right = table[4 * slab + 1, q]
                upper = table[4 * slab + 2, q]
                lower = table[4 * slab + 3, q]

                def of(i):
                    return old[i] if step == 0 else old[i, 0:size]

                e = of(n)
                to_right = pltpu.roll(jnp.where(lane == LANES - 1, of(left), e), 1, 1)
                to_left = pltpu.roll(jnp.where(lane == 0, of(right), e), LANES - 1, 1)
                cy = bank[3, lo:hi]
                moved = (bank[0, lo:hi] * e + bank[1, lo:hi] * of(upper) + bank[2, lo:hi] * of(lower)
                         + jnp.abs(cy) * jnp.where(cy > 0.0, to_right, to_left))
                if step == 3:
                    new[n - shift] = moved
                else:
                    new[n, 0:size] = moved
                return carry

            lax.fori_loop(lead, last + 1, one, 0)
        result(g).start()

    for g in range(len(groups)):
        send_halo(g)
        if g:
            take_halo(g - 1)
            advance_group(g - 1)
    take_halo(len(groups) - 1)
    advance_group(len(groups) - 1)

    def finish(c, carry):
        for j in range(3):
            inward(c, j, True).wait_send()
            for g in range(len(groups)):
                outward(g, c, j, True).wait_send()
        return carry

    lax.fori_loop(0, chunks, finish, 0)
    for way in range(2):
        @pl.when(z < ends if way == 0 else z > 0)
        def _():
            listed(way).wait_send()
            for g in range(len(groups)):
                for part, d in enumerate(peers + (s,)):
                    halo(g, part, d, way).wait_send()

    for g in range(len(groups)):
        result(g).wait()


def expand_kernel(sea, blocks, out, table, sems):
    count = blocks.shape[0]
    rows, per_row = out.shape[1], out.shape[2] // LANES
    for i in range(rows * per_row):
        table[i] = count - 1
    for q in range(count - 1):
        table[lax.div(sea[0, q * LANES], LANES)] = q
    copies = []
    for i in range(rows * per_row):
        row, col = divmod(i, per_row)
        copies.append(pltpu.make_async_copy(
            blocks.at[table[i]], out.at[:, row, col * LANES:(col + 1) * LANES], sems.at[i]))
        copies[-1].start()
    for copy in copies:
        copy.wait()


def fast_body(spectrum, wind, courant, transfer, sea_cells):
    comps, rows, cols = spectrum.shape
    total = transfer.shape[0]
    count = sea_cells.shape[1] // LANES + 1
    chunks = count // 4
    ends = lax.axis_size("space") - 1
    dma = pltpu.SemaphoreType.DMA
    vmem = pl.BlockSpec(memory_space=pltpu.VMEM)
    smem = pl.BlockSpec(memory_space=pltpu.SMEM)
    hbm = pl.BlockSpec(memory_space=pl.ANY)
    f32 = jnp.float32

    blocks, winds, places = pl.pallas_call(
        compact_kernel,
        out_shape=(jax.ShapeDtypeStruct((count, comps, LANES), f32), jax.ShapeDtypeStruct((count, 2, LANES), f32),
                   jax.ShapeDtypeStruct((8 + count, LANES), jnp.int32)),
        in_specs=[smem, hbm, hbm],
        out_specs=(vmem, vmem, vmem),
        scratch_shapes=[dma((count,)), dma((count,))],
        name="compact",
    )(sea_cells, spectrum, wind)

    angle = np.arange(NDIR, dtype=np.float32) * np.float32(2.0 * math.pi / NDIR)
    growth = np.float32(growth_rate) * (np.arange(NFREQ, dtype=np.float32) + 1.0) / NFREQ
    trig = jnp.asarray(np.stack([
        np.repeat(np.cos(angle), NFREQ), np.repeat(np.sin(angle), NFREQ), np.tile(growth, NDIR)], axis=1), f32)

    per_row = cols // LANES
    parts = cuts(comps)
    n = len(parts)
    field = [pltpu.VMEM((3 * count, hi - lo, LANES), f32) for lo, hi in parts]
    made = [pltpu.VMEM((count, hi - lo, LANES), f32) for lo, hi in parts]
    most = max(hi - lo for lo, hi in parts)
    moved = pl.pallas_call(
        lambda *refs: exchange_kernel(ends, per_row, rows * per_row, *refs),
        out_shape=jax.ShapeDtypeStruct((count, comps, LANES), f32),
        in_specs=[vmem, vmem, vmem, vmem, hbm, hbm],
        out_specs=hbm,
        scratch_shapes=field + made + [
            pltpu.VMEM((chunks, 4, comps, LANES), f32),
            pltpu.VMEM((total, LANES), f32),
            pltpu.VMEM((total, LANES), jnp.bfloat16),
            pltpu.VMEM((total, LANES), f32),
            pltpu.VMEM((chunks, 4, comps, LANES), f32),
            pltpu.VMEM(trig.shape, f32),
            pltpu.VMEM(transfer.shape, transfer.dtype),
            pltpu.VMEM((4, comps, LANES), f32),
            pltpu.VMEM((3 * count, most, LANES), f32),
            pltpu.VMEM((3 * count, most, LANES), f32),
            pltpu.VMEM((2, 8 + count, LANES), jnp.int32),
            pltpu.VMEM((16, LANES), jnp.int32),
            pltpu.SMEM((16, LANES), jnp.int32),
            dma((chunks, 3)), dma((chunks, 3)), dma((n, chunks, 3)), dma((n, chunks, 3)),
            dma((n, 2, 4)), dma((n, 2, 4)), dma((chunks,)), dma((n, chunks)),
            dma((2,)), dma((2,)), dma((3,)), dma((n,)),
        ],
        compiler_params=pltpu.CompilerParams(collective_id=0, has_side_effects=True, vmem_limit_bytes=48 << 20),
        name="exchange",
    )(blocks, winds, places, courant.T, trig, transfer)

    return pl.pallas_call(
        expand_kernel,
        out_shape=jax.ShapeDtypeStruct(spectrum.shape, f32),
        in_specs=[smem, vmem],
        out_specs=hbm,
        scratch_shapes=[pltpu.SMEM((rows * per_row,), jnp.int32), dma((rows * per_row,))],
        name="expand",
    )(sea_cells, moved)


def solution(mesh):
    def step(*args):
        if fits(mesh, *args):
            return fast_body(*args)
        return body(*args)

    in_specs = (
        P("spec", "space", None),
        P(None, "space", None),
        P(None, "spec"),
        P(),
        P("space", None),
    )
    out_specs = P("spec", "space", None)
    return jax.shard_map(step, mesh=mesh, in_specs=in_specs, out_specs=out_specs, check_vma=False)
```

```python
import math

import jax
import jax.numpy as jnp
import numpy as np
from jax import lax
from jax.experimental import pallas as pl
from jax.experimental.pallas import tpu as pltpu
from jax.sharding import PartitionSpec as P

NDIR = 36
NFREQ = 36
SUB = 4
SRC_STEPS = 4


growth_rate = 0.05
whitecap = 0.1


def padded_2(cells, sides, width):
    for axis, dim in sides:
        count = lax.axis_size(axis)
        ends = count - 1
        head = lax.slice_in_dim(cells, 0, width, axis=dim)
        tail = lax.slice_in_dim(cells, cells.shape[dim] - width, cells.shape[dim], axis=dim)
        cells = jnp.concatenate(
            [
                lax.ppermute(tail, axis, [(i, (i + 1) % count) for i in range(ends)]),
                cells,
                lax.ppermute(head, axis, [((i + 1) % count, i) for i in range(ends)]),
            ],
            axis=dim,
        )
    return cells


def source_terms(points, wind_pts, transfer):
    angle = jnp.arange(NDIR, dtype=jnp.float32) * (2.0 * math.pi / NDIR)
    cos_comp = jnp.repeat(jnp.cos(angle), NFREQ)
    sin_comp = jnp.repeat(jnp.sin(angle), NFREQ)
    growth = jnp.tile(growth_rate * (jnp.arange(NFREQ, dtype=jnp.float32) + 1.0) / NFREQ, NDIR)
    drive = jnp.maximum(
        cos_comp[:, None] * wind_pts[0][None, :] + sin_comp[:, None] * wind_pts[1][None, :], 0.0
    )
    gamma = growth[:, None] * drive
    for step in range(SRC_STEPS):
        low = points.astype(jnp.bfloat16)
        moved = jnp.dot(transfer, low, preferred_element_type=jnp.float32)
        mean = jnp.mean(points, axis=0, keepdims=True)
        points = points + (gamma - whitecap * mean) * points + moved
    return points


def advance(padded, cx, cy):
    centre = padded[:, 1:-1]
    upper = padded[:, :-2]
    lower = padded[:, 2:]
    left = jnp.roll(centre, 1, axis=2)
    right = jnp.roll(centre, -1, axis=2)
    return (
        centre
        - jnp.maximum(cx, 0.0) * (centre - upper)
        - jnp.minimum(cx, 0.0) * (lower - centre)
        - jnp.maximum(cy, 0.0) * (centre - left)
        - jnp.minimum(cy, 0.0) * (right - centre)
    )


def body(spectrum, wind, courant, transfer, sea_cells):
    comps, rows, cols = spectrum.shape
    cells = rows * cols
    groups = lax.axis_size("spec")
    member = lax.axis_index("spec")
    sea_list = sea_cells[0]
    flat = spectrum.reshape(comps, cells)
    wind_flat = wind.reshape(2, cells)
    mask = jnp.zeros((cells,), jnp.float32).at[sea_list].set(1.0)
    tile = cells // groups
    masked = flat * mask[None, :]
    points = lax.all_to_all(masked, "spec", split_axis=1, concat_axis=0, tiled=True)
    wind_tile = lax.dynamic_slice_in_dim(wind_flat, member * tile, tile, 1)
    updated = source_terms(points, wind_tile, transfer)
    energy = lax.all_to_all(updated, "spec", split_axis=0, concat_axis=1, tiled=True)
    field = energy.reshape(comps, rows, cols)
    cx = courant[0][:, None, None]
    cy = courant[1][:, None, None]
    mask_rows = mask.reshape(1, rows, cols)
    for step in range(SUB):
        padded = padded_2(field, (("space", 1),), 1)
        field = advance(padded, cx, cy) * mask_rows
    return field


LANES = 128
NO_ROW = -5000
NO_COLUMN = -1000
AT_ONCE = 4
GROUP = 56
MESH = pl.DeviceIdType.MESH


def fits(mesh, spectrum, wind, courant, transfer, sea_cells):
    groups = mesh.shape["spec"]
    cells = spectrum.shape[1] * spectrum.shape[2]
    tile = cells // groups
    return (
        groups == 4
        and tile % (8 * LANES) == 0
        and spectrum.shape[2] % LANES == 0
        and sea_cells.shape[1] == 15 * LANES
        and spectrum.shape[1] == SUB
    )


def compact_kernel(sea, spectrum, wind, blocks, winds, places, sem, wind_sem):
    per_row = spectrum.shape[2] // LANES
    count = blocks.shape[0]
    lane = lax.broadcasted_iota(jnp.int32, (8, LANES), 1)
    across = jnp.full((8, LANES), NO_ROW, jnp.int32)
    down = []
    copies = []
    for q in range(count - 1):
        place = lax.div(sea[0, q * LANES], LANES)
        row = lax.div(place, per_row)
        col = pl.multiple_of(lax.rem(place, per_row) * LANES, LANES)
        copies.append(pltpu.make_async_copy(spectrum.at[:, row, pl.ds(col, LANES)], blocks.at[q], sem.at[q]))
        copies.append(pltpu.make_async_copy(wind.at[:, row, pl.ds(col, LANES)], winds.at[q], wind_sem.at[q]))
        copies[-2].start()
        copies[-1].start()
        across = jnp.where(lane == q, place, across)
        places[8 + q:9 + q, :] = jnp.full((1, LANES), place, jnp.int32)
    places[0:8, :] = across
    places[7 + count:8 + count, :] = jnp.full((1, LANES), NO_COLUMN, jnp.int32)
    blocks[count - 1] = jnp.zeros(blocks.shape[1:], blocks.dtype)
    winds[count - 1] = jnp.zeros(winds.shape[1:], winds.dtype)
    for copy in copies:
        copy.wait()


def relatives(s):
    return (s + 1 - 2 * lax.rem(s, 2), lax.rem(s + 2, 4), 3 - s)


def cuts(comps):
    starts = list(range(0, comps - GROUP // 2, GROUP))
    return list(zip(starts, starts[1:] + [comps]))


def exchange_kernel(ends, per_row, span, blocks, winds_hbm, places_hbm, coef_hbm, trig_hbm, transfer_hbm, out, *scratch):
    groups = cuts(blocks.shape[1])
    fields = scratch[:len(groups)]
    results = scratch[len(groups):2 * len(groups)]
    (came, points, low, gamma, made, trig, transfer, winds, places, coef, bank, first, second, lists, found, table,
     in_send, in_recv, out_send, out_recv, halo_send, halo_recv, own_sem, kept_sem,
     list_send, list_recv, load_sem, result_sem) = scratch[2 * len(groups):]
    s = lax.axis_index("spec")
    z = lax.axis_index("space")
    peers = relatives(s)
    comps = blocks.shape[1]
    count = blocks.shape[0]
    chunks = count // 4
    total = points.shape[0]

    barrier = pltpu.get_barrier_semaphore()
    for peer in peers:
        pl.semaphore_signal(barrier, inc=1, device_id={"spec": peer}, device_id_type=MESH)

    @pl.when(z > 0)
    def _():
        pl.semaphore_signal(barrier, inc=1, device_id={"space": z - 1}, device_id_type=MESH)

    @pl.when(z < ends)
    def _():
        pl.semaphore_signal(barrier, inc=1, device_id={"space": z + 1}, device_id_type=MESH)

    pl.semaphore_wait(barrier, 3 + jnp.minimum(z, 1) + jnp.minimum(ends - z, 1))

    def inward(c, j, sending):
        source = blocks.at[chunks * peers[j] + c]
        target = came.at[c, s if sending else peers[j]]
        return pltpu.make_async_remote_copy(
            src_ref=source, dst_ref=target, send_sem=in_send.at[c, j], recv_sem=in_recv.at[c, j],
            device_id={"spec": peers[j]}, device_id_type=MESH)

    def outward(g, c, j, sending):
        source = made.at[c, peers[j], pl.ds(groups[g][0], groups[g][1] - groups[g][0])]
        target = fields[g].at[count + chunks * (s if sending else peers[j]) + c]
        return pltpu.make_async_remote_copy(
            src_ref=source, dst_ref=target, send_sem=out_send.at[g, c, j], recv_sem=out_recv.at[g, c, j],
            device_id={"spec": peers[j]}, device_id_type=MESH)

    def own(c):
        return pltpu.make_async_copy(blocks.at[chunks * s + c], came.at[c, s], own_sem.at[c])

    def kept(g, c):
        source = made.at[c, s, pl.ds(groups[g][0], groups[g][1] - groups[g][0])]
        return pltpu.make_async_copy(source, fields[g].at[count + chunks * s + c], kept_sem.at[g, c])

    def halo(g, part, d, way):
        return pltpu.make_async_remote_copy(
            src_ref=fields[g].at[pl.ds(count + chunks * d, chunks)],
            dst_ref=fields[g].at[pl.ds(2 * way * count + chunks * d, chunks)],
            send_sem=halo_send.at[g, way, part], recv_sem=halo_recv.at[g, way, part],
            device_id={"space": z + 1 - 2 * way}, device_id_type=MESH)

    def listed(way):
        return pltpu.make_async_remote_copy(
            src_ref=places_hbm, dst_ref=lists.at[way], send_sem=list_send.at[way], recv_sem=list_recv.at[way],
            device_id={"space": z + 1 - 2 * way}, device_id_type=MESH)

    def result(g):
        lo, hi = groups[g]
        return pltpu.make_async_copy(results[g], out.at[:, pl.ds(lo, hi - lo)], result_sem.at[g])

    loads = [pltpu.make_async_copy(source, target, load_sem.at[i]) for i, (source, target) in enumerate((
        (places_hbm, places), (coef_hbm, coef), (winds_hbm, winds), (trig_hbm, trig), (transfer_hbm, transfer)))]

    @pl.when(z < ends)
    def _():
        listed(0).start()

    @pl.when(z > 0)
    def _():
        listed(1).start()

    for c in range(chunks):
        for j in (2, 0, 1):
            inward(c, j, True).start()
    for c in range(chunks):
        own(c).start()

    for load in loads:
        load.start()

    @pl.when(z == 0)
    def _():
        for field in fields:
            field[0:count] = jnp.zeros((count,) + field.shape[1:], field.dtype)

    @pl.when(z == ends)
    def _():
        for field in fields:
            field[2 * count:3 * count] = jnp.zeros((count,) + field.shape[1:], field.dtype)

    wide = (comps, LANES)
    loads[0].wait()
    loads[1].wait()
    cx = jnp.broadcast_to(coef[0:1, :], wide[::-1]).T
    cy = jnp.broadcast_to(coef[1:2, :], wide[::-1]).T
    bank[0] = 1.0 - jnp.abs(cx) - jnp.abs(cy)
    bank[1] = jnp.maximum(cx, 0.0)
    bank[2] = -jnp.minimum(cx, 0.0)
    bank[3] = cy

    @pl.when(z < ends)
    def _():
        listed(1).wait_recv()

    @pl.when(z > 0)
    def _():
        listed(0).wait_recv()

    slabs = []
    for slab in range(3):
        if slab == 1:
            across, down = places[0:8, :], places[8:8 + count, :]
        else:
            there = z > 0 if slab == 0 else z < ends
            side = lists[slab // 2]
            across = jnp.where(there, side[0:8, :], NO_ROW)
            down = jnp.where(there, side[8:8 + count, :], NO_COLUMN)
        slabs.append((across, down + slab * span))
    empty = 2 * count - 1
    sub = lax.broadcasted_iota(jnp.int32, (count, LANES), 0)
    at = lax.div(lax.broadcasted_iota(jnp.int32, (1, LANES), 1), count)
    tables = [jnp.full((1, LANES), empty, jnp.int32)] * 4
    for slab, (across, _) in enumerate(slabs):
        place = across[0:1, :]
        col = lax.rem(place, per_row)
        base = place - col + slab * span
        goals = (base + lax.rem(col + per_row - 1, per_row), base + lax.rem(col + 1, per_row),
                 base + col - per_row, base + col + per_row)
        for k, goal in enumerate(goals):
            index = jnp.full((1, LANES), empty, jnp.int32)
            for other, (_, down) in enumerate(slabs):
                hit = jnp.where(down == goal, sub + (other * count - empty), 0)
                index = index + jnp.sum(hit, axis=0, keepdims=True)
            moved = pltpu.roll(jnp.broadcast_to(index, (8, LANES)), slab * count, 1)[0:1, :] if slab else index
            tables[k] = jnp.where(at == slab, moved, tables[k])
    for k in range(4):
        found[k:k + 1, :] = tables[k]
    found[4:8, :] = jnp.full((4, LANES), empty, jnp.int32)
    to_table = pltpu.make_async_copy(found, table, load_sem.at[5])
    to_table.start()
    to_table.wait()
    for load in loads[2:]:
        load.wait()

    def chunk(c, carry):
        own(c).wait()
        for j in range(3):
            inward(c, j, False).wait_recv()
        for p in range(4):
            points[p * comps:(p + 1) * comps, :] = came[c, p]
        pair = winds[chunks * s + c]
        drive = jnp.maximum(trig[:, 0:1] * pair[0:1, :] + trig[:, 1:2] * pair[1:2, :], 0.0)
        gamma[...] = trig[:, 2:3] * drive

        def source(step, carry):
            e = points[...]
            low[...] = e.astype(jnp.bfloat16)
            mean = jnp.sum(e, axis=0, keepdims=True) * (1.0 / total)
            moved = jnp.dot(transfer[...], low[...], preferred_element_type=jnp.float32)
            points[...] = e + (gamma[...] - whitecap * mean) * e + moved
            return carry

        lax.fori_loop(0, SRC_STEPS, source, 0)
        for p in range(4):
            made[c, p] = points[p * comps:(p + 1) * comps, :]
        for j in (2, 0, 1):
            outward(0, c, j, True).start()
        kept(0, c).start()
        return carry

    lax.fori_loop(0, chunks, chunk, 0)

    for g in range(1, len(groups)):
        def send(c, carry, g=g):
            for j in (2, 0, 1):
                outward(g, c, j, True).start()
            kept(g, c).start()
            return carry

        lax.fori_loop(0, chunks, send, 0)

    def send_halo(g):
        def send(part, d):
            @pl.when(z < ends)
            def _():
                halo(g, part, d, 0).start()

            @pl.when(z > 0)
            def _():
                halo(g, part, d, 1).start()

        for c in range(chunks):
            kept(g, c).wait()
        send(3, s)
        for j in range(3):
            for c in range(chunks):
                outward(g, c, j, False).wait_recv()
            send(j, peers[j])

    def take_halo(g):
        for part, d in enumerate(peers + (s,)):
            @pl.when(z < ends)
            def _():
                halo(g, part, d, 1).wait_recv()

            @pl.when(z > 0)
            def _():
                halo(g, part, d, 0).wait_recv()

    def advance_group(g):
        lo, hi = groups[g]
        size = hi - lo
        lane = lax.broadcasted_iota(jnp.int32, (size, LANES), 1)
        for step, lead in enumerate((1, 3, 7, count)):
            old = (fields[g], first, second, first)[step]
            new = (first, second, first, results[g])[step]
            due = 3 * count - 2 * lead if step < 3 else count
            trips = -(-due // AT_ONCE)
            start = (3 * count - trips * AT_ONCE) // 2

            def some(trip, carry):
                def of(i):
                    return old[i] if step == 0 else old[i, 0:size]

                cy = bank[3, lo:hi]
                results_here = []
                for k in range(AT_ONCE):
                    n = start + trip * AT_ONCE + k
                    e = of(n)
                    to_right = pltpu.roll(jnp.where(lane == LANES - 1, of(table[0, n]), e), 1, 1)
                    to_left = pltpu.roll(jnp.where(lane == 0, of(table[1, n]), e), LANES - 1, 1)
                    results_here.append(
                        (n, bank[0, lo:hi] * e + bank[1, lo:hi] * of(table[2, n]) + bank[2, lo:hi] * of(table[3, n])
                         + jnp.abs(cy) * jnp.where(cy > 0.0, to_right, to_left)))
                for n, moved in results_here:
                    if step == 3:
                        new[n - count] = moved
                    else:
                        new[n, 0:size] = moved
                return carry

            lax.fori_loop(0, trips, some, 0)
        result(g).start()

    for g in range(len(groups)):
        send_halo(g)
        if g:
            take_halo(g - 1)
            advance_group(g - 1)
    take_halo(len(groups) - 1)
    advance_group(len(groups) - 1)

    def finish(c, carry):
        for j in range(3):
            inward(c, j, True).wait_send()
            for g in range(len(groups)):
                outward(g, c, j, True).wait_send()
        return carry

    lax.fori_loop(0, chunks, finish, 0)
    for way in range(2):
        @pl.when(z < ends if way == 0 else z > 0)
        def _():
            listed(way).wait_send()
            for g in range(len(groups)):
                for part, d in enumerate(peers + (s,)):
                    halo(g, part, d, way).wait_send()

    for g in range(len(groups)):
        result(g).wait()


def expand_kernel(sea, blocks, out, table, sems):
    count = blocks.shape[0]
    rows, per_row = out.shape[1], out.shape[2] // LANES
    for i in range(rows * per_row):
        table[i] = count - 1
    for q in range(count - 1):
        table[lax.div(sea[0, q * LANES], LANES)] = q
    copies = []
    for i in range(rows * per_row):
        row, col = divmod(i, per_row)
        copies.append(pltpu.make_async_copy(
            blocks.at[table[i]], out.at[:, row, col * LANES:(col + 1) * LANES], sems.at[i]))
        copies[-1].start()
    for copy in copies:
        copy.wait()


def fast_body(spectrum, wind, courant, transfer, sea_cells):
    comps, rows, cols = spectrum.shape
    total = transfer.shape[0]
    count = sea_cells.shape[1] // LANES + 1
    chunks = count // 4
    ends = lax.axis_size("space") - 1
    dma = pltpu.SemaphoreType.DMA
    vmem = pl.BlockSpec(memory_space=pltpu.VMEM)
    smem = pl.BlockSpec(memory_space=pltpu.SMEM)
    hbm = pl.BlockSpec(memory_space=pl.ANY)
    f32 = jnp.float32

    blocks, winds, places = pl.pallas_call(
        compact_kernel,
        out_shape=(jax.ShapeDtypeStruct((count, comps, LANES), f32), jax.ShapeDtypeStruct((count, 2, LANES), f32),
                   jax.ShapeDtypeStruct((8 + count, LANES), jnp.int32)),
        in_specs=[smem, hbm, hbm],
        out_specs=(vmem, vmem, vmem),
        scratch_shapes=[dma((count,)), dma((count,))],
        name="compact",
    )(sea_cells, spectrum, wind)

    angle = np.arange(NDIR, dtype=np.float32) * np.float32(2.0 * math.pi / NDIR)
    growth = np.float32(growth_rate) * (np.arange(NFREQ, dtype=np.float32) + 1.0) / NFREQ
    trig = jnp.asarray(np.stack([
        np.repeat(np.cos(angle), NFREQ), np.repeat(np.sin(angle), NFREQ), np.tile(growth, NDIR)], axis=1), f32)

    per_row = cols // LANES
    parts = cuts(comps)
    n = len(parts)
    field = [pltpu.VMEM((3 * count, hi - lo, LANES), f32) for lo, hi in parts]
    made = [pltpu.VMEM((count, hi - lo, LANES), f32) for lo, hi in parts]
    most = max(hi - lo for lo, hi in parts)
    moved = pl.pallas_call(
        lambda *refs: exchange_kernel(ends, per_row, rows * per_row, *refs),
        out_shape=jax.ShapeDtypeStruct((count, comps, LANES), f32),
        in_specs=[hbm] * 6,
        out_specs=hbm,
        scratch_shapes=field + made + [
            pltpu.VMEM((chunks, 4, comps, LANES), f32),
            pltpu.VMEM((total, LANES), f32),
            pltpu.VMEM((total, LANES), jnp.bfloat16),
            pltpu.VMEM((total, LANES), f32),
            pltpu.VMEM((chunks, 4, comps, LANES), f32),
            pltpu.VMEM(trig.shape, f32),
            pltpu.VMEM(transfer.shape, transfer.dtype),
            pltpu.VMEM((count, 2, LANES), f32),
            pltpu.VMEM((8 + count, LANES), jnp.int32),
            pltpu.VMEM(courant.shape, f32),
            pltpu.VMEM((4, comps, LANES), f32),
            pltpu.VMEM((3 * count, most, LANES), f32),
            pltpu.VMEM((3 * count, most, LANES), f32),
            pltpu.VMEM((2, 8 + count, LANES), jnp.int32),
            pltpu.VMEM((8, LANES), jnp.int32),
            pltpu.SMEM((8, LANES), jnp.int32),
            dma((chunks, 3)), dma((chunks, 3)), dma((n, chunks, 3)), dma((n, chunks, 3)),
            dma((n, 2, 4)), dma((n, 2, 4)), dma((chunks,)), dma((n, chunks)),
            dma((2,)), dma((2,)), dma((6,)), dma((n,)),
        ],
        compiler_params=pltpu.CompilerParams(collective_id=0, has_side_effects=True, vmem_limit_bytes=67043328),
        name="exchange",
    )(blocks, winds, places, courant, trig, transfer)

    return pl.pallas_call(
        expand_kernel,
        out_shape=jax.ShapeDtypeStruct(spectrum.shape, f32),
        in_specs=[smem, vmem],
        out_specs=hbm,
        scratch_shapes=[pltpu.SMEM((rows * per_row,), jnp.int32), dma((rows * per_row,))],
        name="expand",
    )(sea_cells, moved)


def solution(mesh):
    def step(*args):
        if fits(mesh, *args):
            return fast_body(*args)
        return body(*args)

    in_specs = (
        P("spec", "space", None),
        P(None, "space", None),
        P(None, "spec"),
        P(),
        P("space", None),
    )
    out_specs = P("spec", "space", None)
    return jax.shard_map(step, mesh=mesh, in_specs=in_specs, out_specs=out_specs, check_vma=False)
```

```python
import math

import jax
import jax.numpy as jnp
import numpy as np
from jax import lax
from jax.experimental import pallas as pl
from jax.experimental.pallas import tpu as pltpu
from jax.sharding import PartitionSpec as P

NDIR = 36
NFREQ = 36
SUB = 4
SRC_STEPS = 4


growth_rate = 0.05
whitecap = 0.1


def padded_2(cells, sides, width):
    for axis, dim in sides:
        count = lax.axis_size(axis)
        ends = count - 1
        head = lax.slice_in_dim(cells, 0, width, axis=dim)
        tail = lax.slice_in_dim(cells, cells.shape[dim] - width, cells.shape[dim], axis=dim)
        cells = jnp.concatenate(
            [
                lax.ppermute(tail, axis, [(i, (i + 1) % count) for i in range(ends)]),
                cells,
                lax.ppermute(head, axis, [((i + 1) % count, i) for i in range(ends)]),
            ],
            axis=dim,
        )
    return cells


def source_terms(points, wind_pts, transfer):
    angle = jnp.arange(NDIR, dtype=jnp.float32) * (2.0 * math.pi / NDIR)
    cos_comp = jnp.repeat(jnp.cos(angle), NFREQ)
    sin_comp = jnp.repeat(jnp.sin(angle), NFREQ)
    growth = jnp.tile(growth_rate * (jnp.arange(NFREQ, dtype=jnp.float32) + 1.0) / NFREQ, NDIR)
    drive = jnp.maximum(
        cos_comp[:, None] * wind_pts[0][None, :] + sin_comp[:, None] * wind_pts[1][None, :], 0.0
    )
    gamma = growth[:, None] * drive
    for step in range(SRC_STEPS):
        low = points.astype(jnp.bfloat16)
        moved = jnp.dot(transfer, low, preferred_element_type=jnp.float32)
        mean = jnp.mean(points, axis=0, keepdims=True)
        points = points + (gamma - whitecap * mean) * points + moved
    return points


def advance(padded, cx, cy):
    centre = padded[:, 1:-1]
    upper = padded[:, :-2]
    lower = padded[:, 2:]
    left = jnp.roll(centre, 1, axis=2)
    right = jnp.roll(centre, -1, axis=2)
    return (
        centre
        - jnp.maximum(cx, 0.0) * (centre - upper)
        - jnp.minimum(cx, 0.0) * (lower - centre)
        - jnp.maximum(cy, 0.0) * (centre - left)
        - jnp.minimum(cy, 0.0) * (right - centre)
    )


def body(spectrum, wind, courant, transfer, sea_cells):
    comps, rows, cols = spectrum.shape
    cells = rows * cols
    groups = lax.axis_size("spec")
    member = lax.axis_index("spec")
    sea_list = sea_cells[0]
    flat = spectrum.reshape(comps, cells)
    wind_flat = wind.reshape(2, cells)
    mask = jnp.zeros((cells,), jnp.float32).at[sea_list].set(1.0)
    tile = cells // groups
    masked = flat * mask[None, :]
    points = lax.all_to_all(masked, "spec", split_axis=1, concat_axis=0, tiled=True)
    wind_tile = lax.dynamic_slice_in_dim(wind_flat, member * tile, tile, 1)
    updated = source_terms(points, wind_tile, transfer)
    energy = lax.all_to_all(updated, "spec", split_axis=0, concat_axis=1, tiled=True)
    field = energy.reshape(comps, rows, cols)
    cx = courant[0][:, None, None]
    cy = courant[1][:, None, None]
    mask_rows = mask.reshape(1, rows, cols)
    for step in range(SUB):
        padded = padded_2(field, (("space", 1),), 1)
        field = advance(padded, cx, cy) * mask_rows
    return field


LANES = 128
NO_ROW = -5000
NO_COLUMN = -1000
AT_ONCE = 4
SHARES = (0.0, 0.22, 0.42, 0.62, 0.79, 0.91)
MESH = pl.DeviceIdType.MESH


def fits(mesh, spectrum, wind, courant, transfer, sea_cells):
    groups = mesh.shape["spec"]
    cells = spectrum.shape[1] * spectrum.shape[2]
    tile = cells // groups
    return (
        groups == 4
        and tile % (8 * LANES) == 0
        and spectrum.shape[2] % LANES == 0
        and sea_cells.shape[1] == 15 * LANES
        and spectrum.shape[1] == SUB
    )


def compact_kernel(sea, spectrum, wind, blocks, winds, places, sem, wind_sem):
    per_row = spectrum.shape[2] // LANES
    count = blocks.shape[0]
    lane = lax.broadcasted_iota(jnp.int32, (8, LANES), 1)
    across = jnp.full((8, LANES), NO_ROW, jnp.int32)
    down = []
    copies = []
    for q in range(count - 1):
        place = lax.div(sea[0, q * LANES], LANES)
        row = lax.div(place, per_row)
        col = pl.multiple_of(lax.rem(place, per_row) * LANES, LANES)
        copies.append(pltpu.make_async_copy(spectrum.at[:, row, pl.ds(col, LANES)], blocks.at[q], sem.at[q]))
        copies.append(pltpu.make_async_copy(wind.at[:, row, pl.ds(col, LANES)], winds.at[q], wind_sem.at[q]))
        copies[-2].start()
        copies[-1].start()
        across = jnp.where(lane == q, place, across)
        places[8 + q:9 + q, :] = jnp.full((1, LANES), place, jnp.int32)
    places[0:8, :] = across
    places[7 + count:8 + count, :] = jnp.full((1, LANES), NO_COLUMN, jnp.int32)
    blocks[count - 1] = jnp.zeros(blocks.shape[1:], blocks.dtype)
    winds[count - 1] = jnp.zeros(winds.shape[1:], winds.dtype)
    for copy in copies:
        copy.wait()


def relatives(s):
    return (s + 1 - 2 * lax.rem(s, 2), lax.rem(s + 2, 4), 3 - s)


def cuts(comps):
    starts = sorted({8 * round(comps * share / 8) for share in SHARES})
    return list(zip(starts, starts[1:] + [comps]))


def exchange_kernel(ends, per_row, span, blocks, winds_hbm, places_hbm, coef_hbm, trig_hbm, transfer_hbm, out, *scratch):
    groups = cuts(blocks.shape[1])
    fields = scratch[:len(groups)]
    results = scratch[len(groups):2 * len(groups)]
    (came, points, low, gamma, made, trig, transfer, winds, places, coef, bank, first, second, lists, found, table,
     in_send, in_recv, out_send, out_recv, halo_send, halo_recv, own_sem, kept_sem,
     list_send, list_recv, load_sem, result_sem) = scratch[2 * len(groups):]
    s = lax.axis_index("spec")
    z = lax.axis_index("space")
    peers = relatives(s)
    comps = blocks.shape[1]
    count = blocks.shape[0]
    chunks = count // 4
    total = points.shape[0]

    barrier = pltpu.get_barrier_semaphore()
    for peer in peers:
        pl.semaphore_signal(barrier, inc=1, device_id={"spec": peer}, device_id_type=MESH)

    @pl.when(z > 0)
    def _():
        pl.semaphore_signal(barrier, inc=1, device_id={"space": z - 1}, device_id_type=MESH)

    @pl.when(z < ends)
    def _():
        pl.semaphore_signal(barrier, inc=1, device_id={"space": z + 1}, device_id_type=MESH)

    pl.semaphore_wait(barrier, 3 + jnp.minimum(z, 1) + jnp.minimum(ends - z, 1))

    def inward(c, j, sending):
        source = blocks.at[chunks * peers[j] + c]
        target = came.at[c, s if sending else peers[j]]
        return pltpu.make_async_remote_copy(
            src_ref=source, dst_ref=target, send_sem=in_send.at[c, j], recv_sem=in_recv.at[c, j],
            device_id={"spec": peers[j]}, device_id_type=MESH)

    def outward(g, c, j, sending):
        source = made.at[c, peers[j], pl.ds(groups[g][0], groups[g][1] - groups[g][0])]
        target = fields[g].at[count + chunks * (s if sending else peers[j]) + c]
        return pltpu.make_async_remote_copy(
            src_ref=source, dst_ref=target, send_sem=out_send.at[g, c, j], recv_sem=out_recv.at[g, c, j],
            device_id={"spec": peers[j]}, device_id_type=MESH)

    def own(c):
        return pltpu.make_async_copy(blocks.at[chunks * s + c], came.at[c, s], own_sem.at[c])

    def kept(g, c):
        source = made.at[c, s, pl.ds(groups[g][0], groups[g][1] - groups[g][0])]
        return pltpu.make_async_copy(source, fields[g].at[count + chunks * s + c], kept_sem.at[g, c])

    def halo(g, part, d, way):
        return pltpu.make_async_remote_copy(
            src_ref=fields[g].at[pl.ds(count + chunks * d, chunks)],
            dst_ref=fields[g].at[pl.ds(2 * way * count + chunks * d, chunks)],
            send_sem=halo_send.at[g, way, part], recv_sem=halo_recv.at[g, way, part],
            device_id={"space": z + 1 - 2 * way}, device_id_type=MESH)

    def listed(way):
        return pltpu.make_async_remote_copy(
            src_ref=places_hbm, dst_ref=lists.at[way], send_sem=list_send.at[way], recv_sem=list_recv.at[way],
            device_id={"space": z + 1 - 2 * way}, device_id_type=MESH)

    def result(g):
        lo, hi = groups[g]
        return pltpu.make_async_copy(results[g], out.at[:, pl.ds(lo, hi - lo)], result_sem.at[g])

    loads = [pltpu.make_async_copy(source, target, load_sem.at[i]) for i, (source, target) in enumerate((
        (places_hbm, places), (coef_hbm, coef), (winds_hbm, winds), (trig_hbm, trig), (transfer_hbm, transfer)))]

    @pl.when(z < ends)
    def _():
        listed(0).start()

    @pl.when(z > 0)
    def _():
        listed(1).start()

    for c in range(chunks):
        for j in (2, 0, 1):
            inward(c, j, True).start()
    for c in range(chunks):
        own(c).start()

    for load in loads:
        load.start()

    @pl.when(z == 0)
    def _():
        for field in fields:
            field[0:count] = jnp.zeros((count,) + field.shape[1:], field.dtype)

    @pl.when(z == ends)
    def _():
        for field in fields:
            field[2 * count:3 * count] = jnp.zeros((count,) + field.shape[1:], field.dtype)

    wide = (comps, LANES)
    loads[0].wait()
    loads[1].wait()
    cx = jnp.broadcast_to(coef[0:1, :], wide[::-1]).T
    cy = jnp.broadcast_to(coef[1:2, :], wide[::-1]).T
    bank[0] = 1.0 - jnp.abs(cx) - jnp.abs(cy)
    bank[1] = jnp.maximum(cx, 0.0)
    bank[2] = -jnp.minimum(cx, 0.0)
    bank[3] = cy

    @pl.when(z < ends)
    def _():
        listed(1).wait_recv()

    @pl.when(z > 0)
    def _():
        listed(0).wait_recv()

    slabs = []
    for slab in range(3):
        if slab == 1:
            across, down = places[0:8, :], places[8:8 + count, :]
        else:
            there = z > 0 if slab == 0 else z < ends
            side = lists[slab // 2]
            across = jnp.where(there, side[0:8, :], NO_ROW)
            down = jnp.where(there, side[8:8 + count, :], NO_COLUMN)
        slabs.append((across, down + slab * span))
    empty = 2 * count - 1
    sub = lax.broadcasted_iota(jnp.int32, (count, LANES), 0)
    at = lax.div(lax.broadcasted_iota(jnp.int32, (1, LANES), 1), count)
    tables = [jnp.full((1, LANES), empty, jnp.int32)] * 4
    for slab, (across, _) in enumerate(slabs):
        place = across[0:1, :]
        col = lax.rem(place, per_row)
        base = place - col + slab * span
        goals = (base + lax.rem(col + per_row - 1, per_row), base + lax.rem(col + 1, per_row),
                 base + col - per_row, base + col + per_row)
        for k, goal in enumerate(goals):
            index = jnp.full((1, LANES), empty, jnp.int32)
            for other, (_, down) in enumerate(slabs):
                hit = jnp.where(down == goal, sub + (other * count - empty), 0)
                index = index + jnp.sum(hit, axis=0, keepdims=True)
            moved = pltpu.roll(jnp.broadcast_to(index, (8, LANES)), slab * count, 1)[0:1, :] if slab else index
            tables[k] = jnp.where(at == slab, moved, tables[k])
    for k in range(4):
        found[k:k + 1, :] = tables[k]
    found[4:8, :] = jnp.full((4, LANES), empty, jnp.int32)
    to_table = pltpu.make_async_copy(found, table, load_sem.at[5])
    to_table.start()
    to_table.wait()
    for load in loads[2:]:
        load.wait()

    def chunk(c, carry):
        own(c).wait()
        for j in range(3):
            inward(c, j, False).wait_recv()
        for p in range(4):
            points[p * comps:(p + 1) * comps, :] = came[c, p]
        pair = winds[chunks * s + c]
        drive = jnp.maximum(trig[:, 0:1] * pair[0:1, :] + trig[:, 1:2] * pair[1:2, :], 0.0)
        gamma[...] = trig[:, 2:3] * drive

        def source(step, carry):
            e = points[...]
            low[...] = e.astype(jnp.bfloat16)
            mean = jnp.sum(e, axis=0, keepdims=True) * (1.0 / total)
            moved = jnp.dot(transfer[...], low[...], preferred_element_type=jnp.float32)
            points[...] = e + (gamma[...] - whitecap * mean) * e + moved
            return carry

        lax.fori_loop(0, SRC_STEPS, source, 0)
        for p in range(4):
            made[c, p] = points[p * comps:(p + 1) * comps, :]
        for j in (2, 0, 1):
            outward(0, c, j, True).start()
        kept(0, c).start()
        return carry

    lax.fori_loop(0, chunks, chunk, 0)

    for g in range(1, len(groups)):
        def send(c, carry, g=g):
            for j in (2, 0, 1):
                outward(g, c, j, True).start()
            kept(g, c).start()
            return carry

        lax.fori_loop(0, chunks, send, 0)

    def send_halo(g):
        def send(part, d):
            @pl.when(z < ends)
            def _():
                halo(g, part, d, 0).start()

            @pl.when(z > 0)
            def _():
                halo(g, part, d, 1).start()

        for c in range(chunks):
            kept(g, c).wait()
        send(3, s)
        for j in range(3):
            for c in range(chunks):
                outward(g, c, j, False).wait_recv()
            send(j, peers[j])

    def take_halo(g):
        for part, d in enumerate(peers + (s,)):
            @pl.when(z < ends)
            def _():
                halo(g, part, d, 1).wait_recv()

            @pl.when(z > 0)
            def _():
                halo(g, part, d, 0).wait_recv()

    def advance_group(g):
        lo, hi = groups[g]
        size = hi - lo
        lane = lax.broadcasted_iota(jnp.int32, (size, LANES), 1)
        for step, lead in enumerate((1, 3, 7, count)):
            old = (fields[g], first, second, first)[step]
            new = (first, second, first, results[g])[step]
            due = 3 * count - 2 * lead if step < 3 else count
            trips = -(-due // AT_ONCE)
            start = (3 * count - trips * AT_ONCE) // 2

            def some(trip, carry):
                def of(i):
                    return old[i] if step == 0 else old[i, 0:size]

                cy = bank[3, lo:hi]
                results_here = []
                for k in range(AT_ONCE):
                    n = start + trip * AT_ONCE + k
                    e = of(n)
                    to_right = pltpu.roll(jnp.where(lane == LANES - 1, of(table[0, n]), e), 1, 1)
                    to_left = pltpu.roll(jnp.where(lane == 0, of(table[1, n]), e), LANES - 1, 1)
                    results_here.append(
                        (n, bank[0, lo:hi] * e + bank[1, lo:hi] * of(table[2, n]) + bank[2, lo:hi] * of(table[3, n])
                         + jnp.abs(cy) * jnp.where(cy > 0.0, to_right, to_left)))
                for n, moved in results_here:
                    if step == 3:
                        new[n - count] = moved
                    else:
                        new[n, 0:size] = moved
                return carry

            lax.fori_loop(0, trips, some, 0)
        result(g).start()

    for g in range(len(groups)):
        send_halo(g)
        if g >= 2:
            take_halo(g - 2)
            advance_group(g - 2)
    for g in range(max(len(groups) - 2, 0), len(groups)):
        take_halo(g)
        advance_group(g)

    def finish(c, carry):
        for j in range(3):
            inward(c, j, True).wait_send()
            for g in range(len(groups)):
                outward(g, c, j, True).wait_send()
        return carry

    lax.fori_loop(0, chunks, finish, 0)
    for way in range(2):
        @pl.when(z < ends if way == 0 else z > 0)
        def _():
            listed(way).wait_send()
            for g in range(len(groups)):
                for part, d in enumerate(peers + (s,)):
                    halo(g, part, d, way).wait_send()

    for g in range(len(groups)):
        result(g).wait()


def expand_kernel(sea, blocks, out, table, sems):
    count = blocks.shape[0]
    rows, per_row = out.shape[1], out.shape[2] // LANES
    for i in range(rows * per_row):
        table[i] = count - 1
    for q in range(count - 1):
        table[lax.div(sea[0, q * LANES], LANES)] = q
    copies = []
    for i in range(rows * per_row):
        row, col = divmod(i, per_row)
        copies.append(pltpu.make_async_copy(
            blocks.at[table[i]], out.at[:, row, col * LANES:(col + 1) * LANES], sems.at[i]))
        copies[-1].start()
    for copy in copies:
        copy.wait()


def fast_body(spectrum, wind, courant, transfer, sea_cells):
    comps, rows, cols = spectrum.shape
    total = transfer.shape[0]
    count = sea_cells.shape[1] // LANES + 1
    chunks = count // 4
    ends = lax.axis_size("space") - 1
    dma = pltpu.SemaphoreType.DMA
    vmem = pl.BlockSpec(memory_space=pltpu.VMEM)
    smem = pl.BlockSpec(memory_space=pltpu.SMEM)
    hbm = pl.BlockSpec(memory_space=pl.ANY)
    f32 = jnp.float32

    blocks, winds, places = pl.pallas_call(
        compact_kernel,
        out_shape=(jax.ShapeDtypeStruct((count, comps, LANES), f32), jax.ShapeDtypeStruct((count, 2, LANES), f32),
                   jax.ShapeDtypeStruct((8 + count, LANES), jnp.int32)),
        in_specs=[smem, hbm, hbm],
        out_specs=(vmem, vmem, vmem),
        scratch_shapes=[dma((count,)), dma((count,))],
        name="compact",
    )(sea_cells, spectrum, wind)

    angle = np.arange(NDIR, dtype=np.float32) * np.float32(2.0 * math.pi / NDIR)
    growth = np.float32(growth_rate) * (np.arange(NFREQ, dtype=np.float32) + 1.0) / NFREQ
    trig = jnp.asarray(np.stack([
        np.repeat(np.cos(angle), NFREQ), np.repeat(np.sin(angle), NFREQ), np.tile(growth, NDIR)], axis=1), f32)

    per_row = cols // LANES
    parts = cuts(comps)
    n = len(parts)
    field = [pltpu.VMEM((3 * count, hi - lo, LANES), f32) for lo, hi in parts]
    made = [pltpu.VMEM((count, hi - lo, LANES), f32) for lo, hi in parts]
    most = max(hi - lo for lo, hi in parts)
    moved = pl.pallas_call(
        lambda *refs: exchange_kernel(ends, per_row, rows * per_row, *refs),
        out_shape=jax.ShapeDtypeStruct((count, comps, LANES), f32),
        in_specs=[hbm] * 6,
        out_specs=hbm,
        scratch_shapes=field + made + [
            pltpu.VMEM((chunks, 4, comps, LANES), f32),
            pltpu.VMEM((total, LANES), f32),
            pltpu.VMEM((total, LANES), jnp.bfloat16),
            pltpu.VMEM((total, LANES), f32),
            pltpu.VMEM((chunks, 4, comps, LANES), f32),
            pltpu.VMEM(trig.shape, f32),
            pltpu.VMEM(transfer.shape, transfer.dtype),
            pltpu.VMEM((count, 2, LANES), f32),
            pltpu.VMEM((8 + count, LANES), jnp.int32),
            pltpu.VMEM(courant.shape, f32),
            pltpu.VMEM((4, comps, LANES), f32),
            pltpu.VMEM((3 * count, most, LANES), f32),
            pltpu.VMEM((3 * count, most, LANES), f32),
            pltpu.VMEM((2, 8 + count, LANES), jnp.int32),
            pltpu.VMEM((8, LANES), jnp.int32),
            pltpu.SMEM((8, LANES), jnp.int32),
            dma((chunks, 3)), dma((chunks, 3)), dma((n, chunks, 3)), dma((n, chunks, 3)),
            dma((n, 2, 4)), dma((n, 2, 4)), dma((chunks,)), dma((n, chunks)),
            dma((2,)), dma((2,)), dma((6,)), dma((n,)),
        ],
        compiler_params=pltpu.CompilerParams(collective_id=0, has_side_effects=True, vmem_limit_bytes=67043328),
        name="exchange",
    )(blocks, winds, places, courant, trig, transfer)

    return pl.pallas_call(
        expand_kernel,
        out_shape=jax.ShapeDtypeStruct(spectrum.shape, f32),
        in_specs=[smem, vmem],
        out_specs=hbm,
        scratch_shapes=[pltpu.SMEM((rows * per_row,), jnp.int32), dma((rows * per_row,))],
        name="expand",
    )(sea_cells, moved)


def solution(mesh):
    def step(*args):
        if fits(mesh, *args):
            return fast_body(*args)
        return body(*args)

    in_specs = (
        P("spec", "space", None),
        P(None, "space", None),
        P(None, "spec"),
        P(),
        P("space", None),
    )
    out_specs = P("spec", "space", None)
    return jax.shard_map(step, mesh=mesh, in_specs=in_specs, out_specs=out_specs, check_vma=False)
```
